512 devices in a mesh: cam: 8 (over y_lo, x), sp: 64 (over z, y_hi, core).
Axes of the slice: x: 4, y: 8 (y_hi: 4, y_lo: 2; y = y_hi * 2 + y_lo), z: 8, core: 2. Of those that a mesh axis runs over, the one named last changes fastest.
Arguments:
- q_self: bfloat16 [8, 2048, 2048], P('cam', 'sp'), may hold values from -8 to 8
- keys: bfloat16 [8, 2048, 2048], P('cam', 'sp'), may hold values from -4 to 4
- values: bfloat16 [8, 2048, 2048], P('cam', 'sp'), may hold values from -4 to 4
- q_cross: bfloat16 [8, 2048, 2048], P('cam', 'sp'), may hold values from -8 to 8
- timestep: int32 [1], replicated, may hold values from 0 to 49
- mod_table: float32 [50, 2, 2048], replicated, may hold values from 0.5 to 3
Outputs:
- block_out: bfloat16 [8, 2048, 2048], P('cam', 'sp')
The draws below stay inside these ranges and needn't reach their ends.
All inputs are finite; a program needn't handle non-finite values.
Results may differ from the reference program's by a relative error of at most 0.0042.
Values may be sent and summed in bfloat16 or wider, within the bound.
No kernel may reach another device: no remote copies, remote signals or barrier semaphores. Data moves between devices by JAX's collectives and lax.ppermute only.
A program may use at most 64 MiB of HBM per device.

```python
import math
import jax
import jax.numpy as jnp
from jax import lax

HEADS = 16
HEAD_DIM = 128
TOK_DEV = 32
STEPS = 50
CAMS = 8
SEQ = 2048
HD = 2048
N_SP = 64


def draw_keys(key, part):
    drawn = jnp.clip(jax.random.normal(jax.random.fold_in(key, 11), (CAMS, SEQ, HD), jnp.float32), -4.0, 4.0)
    return drawn.astype(jnp.bfloat16)


def draw_q_self(key, part):
    drawn = jnp.clip(jax.random.normal(jax.random.fold_in(key, 21), (CAMS, SEQ, HD), jnp.float32), -8.0, 8.0)
    return drawn.astype(jnp.bfloat16)


def draw_q_cross(key, part):
    drawn = jnp.clip(jax.random.normal(jax.random.fold_in(key, 31), (CAMS, SEQ, HD), jnp.float32), -8.0, 8.0)
    return drawn.astype(jnp.bfloat16)


def level_of(stream_key, dims, shards, least, top_value):
    factor_of, own = 1.0, jax.random.fold_in(stream_key, 6)
    for position, parts in shards:
        heights = jnp.exp(jax.random.uniform(jax.random.fold_in(own, position), (parts,), jnp.float32, least / len(shards), top_value / len(shards)))
        factor_of = factor_of * jnp.repeat(heights, dims[position] // parts).reshape([-1 if axis == position else 1 for axis in range(len(dims))])
    return factor_of


def noise(key, shape, deviation, bound, split=(), dtype=jnp.bfloat16):
    factor_of = level_of(key, shape, split, -0.22, 0.18) if split else 1.0
    entries = jax.random.normal(key, shape, jnp.float32) * deviation * factor_of
    return jnp.minimum(jnp.maximum(entries, -bound), bound).astype(dtype)


def setup_inputs(seed: int = 0) -> dict:
    arg_keys = jax.random.split(jax.random.key(seed), 7)
    return {
        "q_self": draw_q_self(jax.random.fold_in(arg_keys[6], 71), 0),
        "keys": draw_keys(jax.random.fold_in(arg_keys[6], 71), 0),
        "values": noise(arg_keys[2], (CAMS, SEQ, HD), 1.0, 4.0, ((0, 8), (1, 64))),
        "q_cross": draw_q_cross(jax.random.fold_in(arg_keys[6], 71), 0),
        "timestep": jax.random.randint(arg_keys[4], (1,), 0, STEPS).astype(jnp.int32),
        "mod_table": jnp.clip(jnp.exp(jax.random.uniform(arg_keys[5], (STEPS, 2, HD), jnp.float32, math.log(0.5), math.log(3.0))), 0.5, 3.0),
    }


def self_attention(q_self, keys, values):
    score_scale = 1.0 / math.sqrt(HEAD_DIM)

    def stack_heads(tensor):
        return tensor.reshape(CAMS, SEQ, HEADS, HEAD_DIM).transpose(0, 2, 1, 3).reshape(CAMS * HEADS, SEQ, HEAD_DIM)

    def per_head(operands):
        query_part, key_part, value_part = operands
        scores = jnp.dot(query_part, key_part.T, preferred_element_type=jnp.float32) * score_scale
        row_peak = lax.optimization_barrier(jnp.max(scores, axis=1))
        weights = jnp.exp(scores - row_peak[:, None])
        totals = lax.optimization_barrier(jnp.sum(weights, axis=1))
        numerator = jnp.dot(weights.astype(jnp.bfloat16), value_part, preferred_element_type=jnp.float32)
        return (numerator / totals[:, None]).astype(jnp.bfloat16)
    result = lax.map(per_head, (stack_heads(q_self), stack_heads(keys), stack_heads(values)))
    return result.reshape(CAMS, HEADS, SEQ, HEAD_DIM).transpose(0, 2, 1, 3).reshape(CAMS, SEQ, HD)

def cross_view(q_cross, keys, values):
    score_scale = 1.0 / math.sqrt(HEAD_DIM)
    shape_five = (CAMS, N_SP, TOK_DEV, HEADS, HEAD_DIM)
    cross_queries = q_cross.reshape(shape_five)
    key_bands = keys.reshape(shape_five)
    value_bands = values.reshape(shape_five)
    near_keys = jnp.concatenate([jnp.roll(key_bands, 1, axis=0), jnp.roll(key_bands, -1, axis=0)], axis=2)
    near_values = jnp.concatenate([jnp.roll(value_bands, 1, axis=0), jnp.roll(value_bands, -1, axis=0)], axis=2)

    def per_camera(operands):
        query_part, key_part, value_part = operands
        scores = jnp.einsum('bqhd,bkhd->bhqk', query_part.astype(jnp.float32), key_part.astype(jnp.float32)) * score_scale
        row_peak = lax.optimization_barrier(jnp.max(scores, axis=3))
        weights = jnp.exp(scores - row_peak[..., None])
        totals = lax.optimization_barrier(jnp.sum(weights, axis=3))
        rounded = lax.optimization_barrier(weights.astype(jnp.bfloat16)).astype(jnp.float32)
        numerator = jnp.einsum('bhqk,bkhd->bqhd', rounded, value_part.astype(jnp.float32))
        return numerator / jnp.swapaxes(totals, 1, 2)[..., None]
    result = lax.map(per_camera, (cross_queries, near_keys, near_values))
    return result.reshape(CAMS, SEQ, HD)

def reference(q_self, keys, values, q_cross, timestep, mod_table):
    self_out = self_attention(q_self, keys, values)
    cross_out = cross_view(q_cross, keys, values)
    gate_rows = mod_table[timestep[0]]
    mixed = gate_rows[0] * self_out.astype(jnp.float32) + gate_rows[1] * cross_out
    return mixed.astype(jnp.bfloat16)
```

```python
import functools
import math

import jax
import jax.numpy as jnp
from jax import lax
from jax.experimental import pallas as pl
from jax.experimental.pallas import tpu as pltpu
from jax.sharding import Mesh
from jax.sharding import PartitionSpec as P

HEADS = 16
LOG2E = 1.4426950408889634

AXES = ("yo", "x", "z", "yh", "yl", "core")
SHAPE = (2, 4, 8, 2, 2, 2)
CAM = ("yo", "x")
SP = ("z", "yh", "yl", "core")
OWNERS = ("z", "yh", "yl")

VMEM = pl.BlockSpec(memory_space=pltpu.VMEM)


def grant(mebibytes):
    return pltpu.CompilerParams(vmem_limit_bytes=mebibytes << 20)


def pack_kernel(q_ref, k_ref, v_ref, piece_ref, near_ref):
    rows = q_ref.shape[0]
    half = rows // 2
    for head in range(HEADS):
        z, yl = divmod(head, 2)
        lanes = slice(head * 128, (head + 1) * 128)
        key = k_ref[:, lanes]
        value = v_ref[:, lanes]
        near_ref[head, :rows, :] = key
        near_ref[head, rows:, :] = value
        for yh in range(2):
            to = (z * 2 + yh) * 2 + yl
            piece_ref[to, :rows, :] = key
            piece_ref[to, rows : 2 * rows, :] = value
            piece_ref[to, 2 * rows :, :] = q_ref[yh * half : (yh + 1) * half, lanes]


def scores_of(query, key):
    return lax.dot_general(query, key, (((1,), (1,)), ((), ())), preferred_element_type=jnp.float32)


def self_kernel(scale, mine_ref, other_ref, out_ref):
    pieces, depth, dim = mine_ref.shape
    part = depth // 5
    block = 8
    keys = [r[:, : 2 * part, :].reshape(pieces * 2 * part, dim) for r in (mine_ref, other_ref)]
    values = [
        r[:, 2 * part : 4 * part, :].reshape(pieces * 2 * part, dim) for r in (mine_ref, other_ref)
    ]
    for start in range(0, pieces, block):
        query = mine_ref[start : start + block, 4 * part :, :].reshape(block * part, dim)
        scores = [scores_of(query, key) for key in keys]
        peak = functools.reduce(
            jnp.maximum, [jnp.max(s, axis=1, keepdims=True) for s in scores]
        )
        weights = [jnp.exp2((s - peak) * scale) for s in scores]
        total = sum(jnp.sum(w, axis=1, keepdims=True) for w in weights)
        numerator = sum(
            jnp.dot(w.astype(jnp.bfloat16), value, preferred_element_type=jnp.float32)
            for w, value in zip(weights, values)
        )
        out_ref[start : start + block] = (
            (numerator / total).astype(jnp.bfloat16).reshape(block, part, dim)
        )


def cross_kernel(scale, step_ref, q_ref, left_ref, right_ref, gate_ref, out_ref):
    rows = q_ref.shape[0]
    for head in range(HEADS):
        lanes = slice(head * 128, (head + 1) * 128)
        query = q_ref[:, lanes]
        left = scores_of(query, left_ref[head, :rows, :])
        right = scores_of(query, right_ref[head, :rows, :])
        peak = jnp.maximum(
            jnp.max(left, axis=1, keepdims=True), jnp.max(right, axis=1, keepdims=True)
        )
        left = jnp.exp2((left - peak) * scale)
        right = jnp.exp2((right - peak) * scale)
        total = jnp.sum(left, axis=1, keepdims=True) + jnp.sum(right, axis=1, keepdims=True)
        numerator = jnp.dot(
            left.astype(jnp.bfloat16), left_ref[head, rows:, :], preferred_element_type=jnp.float32
        ) + jnp.dot(
            right.astype(jnp.bfloat16), right_ref[head, rows:, :], preferred_element_type=jnp.float32
        )
        out_ref[:, lanes] = (numerator / total) * gate_ref[0, 1:2, lanes]


def mix_kernel(step_ref, self_ref, cross_ref, gate_ref, out_ref):
    half = self_ref.shape[1]
    for head in range(HEADS):
        z, yl = divmod(head, 2)
        lanes = slice(head * 128, (head + 1) * 128)
        for yh in range(2):
            rows = slice(yh * half, (yh + 1) * half)
            mine = self_ref[(z * 2 + yh) * 2 + yl].astype(jnp.float32)
            out_ref[0, rows, lanes] = (
                mine * gate_ref[0, 0:1, lanes] + cross_ref[rows, lanes]
            ).astype(jnp.bfloat16)


def shift(value, steps):
    pairs = [(source, (source + steps) % 8) for source in range(8)]
    return lax.ppermute(value, CAM, pairs)


def local(q_self, keys, values, q_cross, timestep, mod_table):
    rows, width = q_self.shape[1:]
    dim = width // HEADS
    scale = LOG2E / math.sqrt(dim)
    full = lambda *shape: pl.BlockSpec(shape, lambda i, step: (0,) * len(shape))
    gates = pl.BlockSpec((1, 2, width), lambda i, step: (step[0], 0, 0))

    pieces, near = pl.pallas_call(
        pack_kernel,
        out_shape=(
            jax.ShapeDtypeStruct((2 * HEADS, 5 * rows // 2, dim), jnp.bfloat16),
            jax.ShapeDtypeStruct((HEADS, 2 * rows, dim), jnp.bfloat16),
        ),
        in_specs=[VMEM] * 3,
        out_specs=(VMEM, VMEM),
        compiler_params=grant(8),
        name="pack",
    )(q_self[0], keys[0], values[0])

    mine = lax.all_to_all(pieces, OWNERS, split_axis=0, concat_axis=0, tiled=True)
    left = shift(near, 1)
    right = shift(near, -1)
    cross = pl.pallas_call(
        functools.partial(cross_kernel, scale),
        out_shape=jax.ShapeDtypeStruct((rows, width), jnp.float32),
        grid_spec=pltpu.PrefetchScalarGridSpec(
            num_scalar_prefetch=1,
            grid=(1,),
            in_specs=[
                full(rows, width),
                full(*near.shape),
                full(*near.shape),
                gates,
            ],
            out_specs=full(rows, width),
        ),
        cost_estimate=pl.CostEstimate(flops=17_000_000, bytes_accessed=900_000, transcendentals=40_000),
        compiler_params=grant(8),
        name="cross",
    )(timestep, q_cross[0], left, right, mod_table)

    other = lax.ppermute(mine, "core", [(0, 1), (1, 0)])
    part = pl.pallas_call(
        functools.partial(self_kernel, scale),
        out_shape=jax.ShapeDtypeStruct((2 * HEADS, rows // 2, dim), jnp.bfloat16),
        in_specs=[VMEM] * 2,
        out_specs=VMEM,
        compiler_params=grant(24),
        name="self",
    )(mine, other)
    own = lax.all_to_all(part, OWNERS, split_axis=0, concat_axis=0, tiled=True)
    return pl.pallas_call(
        mix_kernel,
        out_shape=jax.ShapeDtypeStruct((1, rows, width), jnp.bfloat16),
        grid_spec=pltpu.PrefetchScalarGridSpec(
            num_scalar_prefetch=1,
            grid=(1,),
            in_specs=[full(*own.shape), full(rows, width), gates],
            out_specs=full(1, rows, width),
        ),
        compiler_params=grant(8),
        name="mix",
    )(timestep, own, cross, mod_table)


def solution(mesh):
    fine = Mesh(mesh.devices.reshape(SHAPE), AXES)
    block = P(CAM, SP, None)
    return jax.shard_map(
        local,
        mesh=fine,
        in_specs=(block, block, block, block, P(), P()),
        out_specs=block,
        check_vma=False,
    )
```

```python
import functools
import math

import jax
import jax.numpy as jnp
from jax import lax
from jax.experimental import pallas as pl
from jax.experimental.pallas import tpu as pltpu
from jax.sharding import Mesh
from jax.sharding import PartitionSpec as P

HEADS = 16
LOG2E = 1.4426950408889634

AXES = ("yo", "x", "z", "yh", "yl", "core")
SHAPE = (2, 4, 8, 2, 2, 2)
CAM = ("yo", "x")
SP = ("z", "yh", "yl", "core")
OWNERS = ("z", "yh", "yl")

VMEM = pl.BlockSpec(memory_space=pltpu.VMEM)


def grant(mebibytes):
    return pltpu.CompilerParams(vmem_limit_bytes=mebibytes << 20)


def pack_kernel(q_hbm, k_hbm, v_hbm, piece_ref, near_ref, q_ref, k_ref, v_ref, sems):
    rows = q_ref.shape[0]
    copies = [
        pltpu.make_async_copy(source, target, sems.at[i])
        for i, (source, target) in enumerate(((k_hbm, k_ref), (v_hbm, v_ref), (q_hbm, q_ref)))
    ]
    for copy in copies:
        copy.start()
    for i, (copy, part) in enumerate(zip(copies, (k_ref, v_ref, q_ref))):
        copy.wait()
        to = slice(i * rows, (i + 1) * rows)
        for head in range(HEADS):
            z, yl = divmod(head, 2)
            block = part[:, head * 128 : (head + 1) * 128]
            piece_ref[z * 4 + yl, to, :] = block
            piece_ref[z * 4 + 2 + yl, to, :] = block
            if i < 2:
                near_ref[head, to, :] = block


def scores_of(query, key):
    return lax.dot_general(query, key, (((1,), (1,)), ((), ())), preferred_element_type=jnp.float32)


def self_kernel(scale, yh_ref, mine_ref, other_ref, out_ref):
    lines, _, across, depth, dim = mine_ref.shape
    part = depth // 3
    block = 2
    keys = [r[..., :part, :].reshape(-1, dim) for r in (mine_ref, other_ref)]
    values = [r[..., part : 2 * part, :].reshape(-1, dim) for r in (mine_ref, other_ref)]
    for start in range(0, lines, block):
        query = mine_ref[start : start + block, yh_ref[0], :, 2 * part :, :]
        query = query.reshape(block * across * part, dim)
        scores = [scores_of(query, key) for key in keys]
        peak = functools.reduce(
            jnp.maximum, [jnp.max(s, axis=1, keepdims=True) for s in scores]
        )
        weights = [jnp.exp2((s - peak) * scale) for s in scores]
        total = sum(jnp.sum(w, axis=1, keepdims=True) for w in weights)
        numerator = sum(
            jnp.dot(w.astype(jnp.bfloat16), value, preferred_element_type=jnp.float32)
            for w, value in zip(weights, values)
        )
        out_ref[start * across : (start + block) * across] = (
            (numerator / total).astype(jnp.bfloat16).reshape(block * across, part, dim)
        )


def cross_kernel(scale, step_ref, q_ref, left_ref, right_ref, gate_ref, out_ref):
    rows = q_ref.shape[0]
    for head in range(HEADS):
        lanes = slice(head * 128, (head + 1) * 128)
        query = q_ref[:, lanes]
        left = scores_of(query, left_ref[head, :rows, :])
        right = scores_of(query, right_ref[head, :rows, :])
        peak = jnp.maximum(
            jnp.max(left, axis=1, keepdims=True), jnp.max(right, axis=1, keepdims=True)
        )
        left = jnp.exp2((left - peak) * scale)
        right = jnp.exp2((right - peak) * scale)
        total = jnp.sum(left, axis=1, keepdims=True) + jnp.sum(right, axis=1, keepdims=True)
        numerator = jnp.dot(
            left.astype(jnp.bfloat16), left_ref[head, rows:, :], preferred_element_type=jnp.float32
        ) + jnp.dot(
            right.astype(jnp.bfloat16), right_ref[head, rows:, :], preferred_element_type=jnp.float32
        )
        out_ref[:, lanes] = (numerator / total) * gate_ref[0, 1:2, lanes]


def mix_kernel(step_ref, self_ref, cross_ref, gate_ref, out_ref):
    for head in range(HEADS):
        lanes = slice(head * 128, (head + 1) * 128)
        out_ref[0, :, lanes] = (
            self_ref[head].astype(jnp.float32) * gate_ref[0, 0:1, lanes] + cross_ref[:, lanes]
        ).astype(jnp.bfloat16)


def shift(value, steps):
    pairs = [(source, (source + steps) % 8) for source in range(8)]
    return lax.ppermute(value, CAM, pairs)


def local(q_self, keys, values, q_cross, timestep, mod_table):
    rows, width = q_self.shape[1:]
    dim = width // HEADS
    scale = LOG2E / math.sqrt(dim)
    full = lambda *shape: pl.BlockSpec(shape, lambda i, step: (0,) * len(shape))
    gates = pl.BlockSpec((1, 2, width), lambda i, step: (step[0], 0, 0))

    pieces, near = pl.pallas_call(
        pack_kernel,
        out_shape=(
            jax.ShapeDtypeStruct((2 * HEADS, 3 * rows, dim), jnp.bfloat16),
            jax.ShapeDtypeStruct((HEADS, 2 * rows, dim), jnp.bfloat16),
        ),
        in_specs=[pl.BlockSpec(memory_space=pltpu.HBM)] * 3,
        out_specs=(VMEM, VMEM),
        scratch_shapes=[pltpu.VMEM((rows, width), jnp.bfloat16)] * 3
        + [pltpu.SemaphoreType.DMA((3,))],
        compiler_params=grant(8),
        name="pack",
    )(*(pltpu.with_memory_space_constraint(x[0], pltpu.HBM) for x in (q_self, keys, values)))

    mine = lax.all_to_all(pieces, OWNERS, split_axis=0, concat_axis=0, tiled=True)
    left = shift(near, 1)
    right = shift(near, -1)
    cross = pl.pallas_call(
        functools.partial(cross_kernel, scale),
        out_shape=jax.ShapeDtypeStruct((rows, width), jnp.float32),
        grid_spec=pltpu.PrefetchScalarGridSpec(
            num_scalar_prefetch=1,
            grid=(1,),
            in_specs=[full(rows, width), full(*near.shape), full(*near.shape), gates],
            out_specs=full(rows, width),
        ),
        compiler_params=grant(8),
        name="cross",
    )(timestep, q_cross[0], left, right, mod_table)
    other = lax.ppermute(mine[:, : 2 * rows], "core", [(0, 1), (1, 0)])
    whole = lambda *shape: pl.BlockSpec(shape, lambda i, yh: (0,) * len(shape))
    part = pl.pallas_call(
        functools.partial(self_kernel, scale),
        out_shape=jax.ShapeDtypeStruct((HEADS, rows, dim), jnp.bfloat16),
        grid_spec=pltpu.PrefetchScalarGridSpec(
            num_scalar_prefetch=1,
            grid=(1,),
            in_specs=[whole(8, 2, 2, 3 * rows, dim), whole(8, 2, 2, 2 * rows, dim)],
            out_specs=whole(HEADS, rows, dim),
        ),
        compiler_params=grant(24),
        name="self",
    )(
        lax.axis_index("yh")[None],
        mine.reshape(8, 2, 2, 3 * rows, dim),
        other.reshape(8, 2, 2, 2 * rows, dim),
    )
    own = lax.all_to_all(part, ("z", "yl"), split_axis=0, concat_axis=0, tiled=True)
    return pl.pallas_call(
        mix_kernel,
        out_shape=jax.ShapeDtypeStruct((1, rows, width), jnp.bfloat16),
        grid_spec=pltpu.PrefetchScalarGridSpec(
            num_scalar_prefetch=1,
            grid=(1,),
            in_specs=[full(*own.shape), full(rows, width), gates],
            out_specs=full(1, rows, width),
        ),
        compiler_params=grant(8),
        name="mix",
    )(timestep, own, cross, mod_table)


def solution(mesh):
    fine = Mesh(mesh.devices.reshape(SHAPE), AXES)
    block = P(CAM, SP, None)
    return jax.shard_map(
        local,
        mesh=fine,
        in_specs=(block, block, block, block, P(), P()),
        out_specs=block,
        check_vma=False,
    )
```

```python
import functools
import math

import jax
import jax.numpy as jnp
from jax import lax
from jax.experimental import pallas as pl
from jax.experimental.pallas import tpu as pltpu
from jax.sharding import Mesh
from jax.sharding import PartitionSpec as P

HEADS = 16
LOG2E = 1.4426950408889634

AXES = ("yo", "x", "z", "yh", "yl", "core")
SHAPE = (2, 4, 8, 2, 2, 2)
CAM = ("yo", "x")
SP = ("z", "yh", "yl", "core")
OWNERS = ("z", "yh", "yl")

VMEM = pl.BlockSpec(memory_space=pltpu.VMEM)


def grant(mebibytes):
    return pltpu.CompilerParams(vmem_limit_bytes=mebibytes << 20)


def pack_kernel(q_hbm, k_hbm, v_hbm, piece_ref, near_ref, q_ref, k_ref, v_ref, sems):
    rows = q_ref.shape[0]
    copies = [
        pltpu.make_async_copy(source, target, sems.at[i])
        for i, (source, target) in enumerate(((k_hbm, k_ref), (v_hbm, v_ref), (q_hbm, q_ref)))
    ]
    for copy in copies:
        copy.start()
    for i, (copy, part) in enumerate(zip(copies, (k_ref, v_ref, q_ref))):
        copy.wait()
        to = slice(i * rows, (i + 1) * rows)
        for head in range(HEADS):
            z, yl = divmod(head, 2)
            block = part[:, head * 128 : (head + 1) * 128]
            piece_ref[z * 4 + yl, to, :] = block
            piece_ref[z * 4 + 2 + yl, to, :] = block
            if i < 2:
                near_ref[head, to, :] = block


def pick_kernel(step_ref, table_ref, out_ref, sem):
    copy = pltpu.make_async_copy(table_ref.at[step_ref[0]], out_ref, sem)
    copy.start()
    copy.wait()


def scores_of(query, key):
    return lax.dot_general(query, key, (((1,), (1,)), ((), ())), preferred_element_type=jnp.float32)


def self_kernel(scale, yh_ref, mine_ref, other_ref, out_ref):
    lines, _, across, depth, dim = mine_ref.shape
    part = depth // 3
    block = 2
    keys = [r[..., :part, :].reshape(-1, dim) for r in (mine_ref, other_ref)]
    values = [r[..., part : 2 * part, :].reshape(-1, dim) for r in (mine_ref, other_ref)]
    values = [jnp.concatenate([value, jnp.ones_like(value)], axis=1) for value in values]
    for start in range(0, lines, block):
        query = mine_ref[start : start + block, yh_ref[0], :, 2 * part :, :]
        query = query.reshape(block * across * part, dim)
        scores = [scores_of(query, key) for key in keys]
        peak = functools.reduce(
            jnp.maximum, [jnp.max(s, axis=1, keepdims=True) for s in scores]
        )
        summed = sum(
            jnp.dot(
                jnp.exp2((s - peak) * scale).astype(jnp.bfloat16),
                value,
                preferred_element_type=jnp.float32,
            )
            for s, value in zip(scores, values)
        )
        out_ref[start * across : (start + block) * across] = (
            (summed[:, :dim] / summed[:, dim:])
            .astype(jnp.bfloat16)
            .reshape(block * across, part, dim)
        )


def cross_kernel(scale, q_ref, left_ref, right_ref, gate_ref, out_ref):
    rows = q_ref.shape[0]
    both = lambda head, part: jnp.concatenate([left_ref[head, part], right_ref[head, part]], axis=0)
    lanes = [slice(head * 128, (head + 1) * 128) for head in range(HEADS)]
    scores = jnp.concatenate(
        [scores_of(q_ref[:, lanes[head]], both(head, slice(rows))) for head in range(HEADS)],
        axis=0,
    )
    weights = jnp.exp2((scores - jnp.max(scores, axis=1, keepdims=True)) * scale)
    inverse = 1.0 / jnp.sum(weights, axis=1, keepdims=True)
    weights = weights.astype(jnp.bfloat16)
    for head in range(HEADS):
        at = slice(head * rows, (head + 1) * rows)
        numerator = jnp.dot(
            weights[at], both(head, slice(rows, None)), preferred_element_type=jnp.float32
        )
        out_ref[:, lanes[head]] = numerator * (inverse[at] * gate_ref[1:2, lanes[head]])


def mix_kernel(self_ref, cross_ref, gate_ref, out_ref):
    for head in range(HEADS):
        lanes = slice(head * 128, (head + 1) * 128)
        out_ref[0, :, lanes] = (
            self_ref[head].astype(jnp.float32) * gate_ref[0:1, lanes] + cross_ref[:, lanes]
        ).astype(jnp.bfloat16)


def shift(value, steps):
    pairs = [(source, (source + steps) % 8) for source in range(8)]
    return lax.ppermute(value, CAM, pairs)


def local(q_self, keys, values, q_cross, timestep, mod_table):
    rows, width = q_self.shape[1:]
    dim = width // HEADS
    scale = LOG2E / math.sqrt(dim)
    pieces, near = pl.pallas_call(
        pack_kernel,
        out_shape=(
            jax.ShapeDtypeStruct((2 * HEADS, 3 * rows, dim), jnp.bfloat16),
            jax.ShapeDtypeStruct((HEADS, 2 * rows, dim), jnp.bfloat16),
        ),
        in_specs=[pl.BlockSpec(memory_space=pltpu.HBM)] * 3,
        out_specs=(VMEM, VMEM),
        scratch_shapes=[pltpu.VMEM((rows, width), jnp.bfloat16)] * 3
        + [pltpu.SemaphoreType.DMA((3,))],
        compiler_params=grant(8),
        name="pack",
    )(*(pltpu.with_memory_space_constraint(x[0], pltpu.HBM) for x in (q_self, keys, values)))

    mine = lax.all_to_all(pieces, OWNERS, split_axis=0, concat_axis=0, tiled=True)
    left = shift(near, 1)
    right = shift(near, -1)
    gates = pl.pallas_call(
        pick_kernel,
        out_shape=jax.ShapeDtypeStruct((2, width), jnp.float32),
        in_specs=[pl.BlockSpec(memory_space=pltpu.SMEM), pl.BlockSpec(memory_space=pltpu.HBM)],
        out_specs=VMEM,
        scratch_shapes=[pltpu.SemaphoreType.DMA],
        compiler_params=grant(1),
        name="pick",
    )(timestep, pltpu.with_memory_space_constraint(mod_table, pltpu.HBM))
    cross = pl.pallas_call(
        functools.partial(cross_kernel, scale),
        out_shape=jax.ShapeDtypeStruct((rows, width), jnp.float32),
        in_specs=[VMEM] * 4,
        out_specs=VMEM,
        compiler_params=grant(8),
        name="cross",
    )(q_cross[0], left, right, gates)
    other = lax.ppermute(mine[:, : 2 * rows], "core", [(0, 1), (1, 0)])
    whole = lambda *shape: pl.BlockSpec(shape, lambda i, yh: (0,) * len(shape))
    part = pl.pallas_call(
        functools.partial(self_kernel, scale),
        out_shape=jax.ShapeDtypeStruct((HEADS, rows, dim), jnp.bfloat16),
        grid_spec=pltpu.PrefetchScalarGridSpec(
            num_scalar_prefetch=1,
            grid=(1,),
            in_specs=[whole(8, 2, 2, 3 * rows, dim), whole(8, 2, 2, 2 * rows, dim)],
            out_specs=whole(HEADS, rows, dim),
        ),
        compiler_params=grant(24),
        name="self",
    )(
        lax.axis_index("yh")[None],
        mine.reshape(8, 2, 2, 3 * rows, dim),
        other.reshape(8, 2, 2, 2 * rows, dim),
    )
    own = lax.all_to_all(part, ("z", "yl"), split_axis=0, concat_axis=0, tiled=True)
    return pl.pallas_call(
        mix_kernel,
        out_shape=jax.ShapeDtypeStruct((1, rows, width), jnp.bfloat16),
        in_specs=[VMEM] * 3,
        out_specs=VMEM,
        compiler_params=grant(8),
        name="mix",
    )(own, cross, gates)


def solution(mesh):
    fine = Mesh(mesh.devices.reshape(SHAPE), AXES)
    block = P(CAM, SP, None)
    return jax.shard_map(
        local,
        mesh=fine,
        in_specs=(block, block, block, block, P(), P()),
        out_specs=block,
        check_vma=False,
    )
```

```python
import functools
import math

import jax
import jax.numpy as jnp
from jax import lax
from jax.experimental import pallas as pl
from jax.experimental.pallas import tpu as pltpu
from jax.sharding import PartitionSpec as P

HEADS = 16
LOG2E = 1.4426950408889634

IN_Z, IN_YH, IN_YL = (5, 6, 7, 0, 1, 2, 3, 4), 1, 0
OUT_Z, OUT_YL = (4, 5, 6, 7, 0, 1, 2, 3), 1


def place(z, yh, yl, core):
    return ((z * 2 + yh) * 2 + yl) * 2 + core


def owners():
    return [
        [
            place(z, yh ^ IN_YH, yl ^ IN_YL, core)
            for z in IN_Z
            for yh in range(2)
            for yl in range(2)
        ]
        for core in range(2)
    ]


def half_owners():
    return [
        [place(z, yh, yl ^ OUT_YL, core) for z in OUT_Z for yl in range(2)]
        for yh in range(2)
        for core in range(2)
    ]


def seat(z, yl):
    return OUT_Z.index(z) * 2 + (yl ^ OUT_YL)


VMEM = pl.BlockSpec(memory_space=pltpu.VMEM)


def grant(mebibytes):
    return pltpu.CompilerParams(vmem_limit_bytes=mebibytes << 20)


def pack_kernel(q_hbm, k_hbm, v_hbm, piece_ref, near_ref, q_ref, k_ref, v_ref, sems):
    rows = q_ref.shape[0]
    copies = [
        pltpu.make_async_copy(source, target, sems.at[i])
        for i, (source, target) in enumerate(((k_hbm, k_ref), (v_hbm, v_ref), (q_hbm, q_ref)))
    ]
    for copy in copies:
        copy.start()
    for i, (copy, part) in enumerate(zip(copies, (k_ref, v_ref, q_ref))):
        copy.wait()
        to = slice(i * rows, (i + 1) * rows)
        for head in range(HEADS):
            z, yl = divmod(head, 2)
            line, side = IN_Z.index(z), yl ^ IN_YL
            block = part[:, head * 128 : (head + 1) * 128]
            piece_ref[line * 4 + side, to, :] = block
            piece_ref[line * 4 + 2 + side, to, :] = block
            if i < 2:
                near_ref[head, to, :] = block


def pick_kernel(step_ref, table_ref, out_ref, sem):
    copy = pltpu.make_async_copy(table_ref.at[step_ref[0]], out_ref, sem)
    copy.start()
    copy.wait()


def scores_of(query, key):
    return lax.dot_general(query, key, (((1,), (1,)), ((), ())), preferred_element_type=jnp.float32)


def self_kernel(scale, yh_ref, mine_ref, other_ref, out_ref):
    depths, _, across, depth, dim = mine_ref.shape
    part = depth // 3
    block = 4
    keys = [r[..., :part, :].reshape(-1, dim) for r in (mine_ref, other_ref)]
    values = [r[..., part : 2 * part, :].reshape(-1, dim) for r in (mine_ref, other_ref)]
    values = [jnp.concatenate([value, jnp.ones_like(value)], axis=1) for value in values]

    def scored(start):
        query = mine_ref[start : start + block, yh_ref[0], :, 2 * part :, :]
        query = query.reshape(block * across * part, dim)
        return [scores_of(query, key) for key in keys]

    ahead = scored(0)
    for start in range(0, depths, block):
        scores = ahead
        if start + block < depths:
            ahead = scored(start + block)
        peak = functools.reduce(
            jnp.maximum, [jnp.max(s, axis=1, keepdims=True) for s in scores]
        )
        weights = [jnp.exp2((s - peak) * scale).astype(jnp.bfloat16) for s in scores]
        summed = sum(
            jnp.dot(weight, value, preferred_element_type=jnp.float32)
            for weight, value in zip(weights, values)
        )
        mixed = (summed[:, :dim] / summed[:, dim:]).astype(jnp.bfloat16)
        for i in range(block * across):
            line, side = divmod(start * across + i, across)
            out_ref[seat(IN_Z[line], side ^ IN_YL)] = mixed[i * part : (i + 1) * part]


def cross_kernel(scale, q_ref, left_ref, right_ref, gate_ref, out_ref):
    rows = q_ref.shape[0]
    both = lambda head, part: jnp.concatenate([left_ref[head, part], right_ref[head, part]], axis=0)
    lanes = [slice(head * 128, (head + 1) * 128) for head in range(HEADS)]
    scores = jnp.concatenate(
        [scores_of(q_ref[:, lanes[head]], both(head, slice(rows))) for head in range(HEADS)],
        axis=0,
    )
    weights = jnp.exp2((scores - jnp.max(scores, axis=1, keepdims=True)) * scale)
    inverse = 1.0 / jnp.sum(weights, axis=1, keepdims=True)
    weights = weights.astype(jnp.bfloat16)
    for head in range(HEADS):
        at = slice(head * rows, (head + 1) * rows)
        numerator = jnp.dot(
            weights[at], both(head, slice(rows, None)), preferred_element_type=jnp.float32
        )
        out_ref[:, lanes[head]] = numerator * (inverse[at] * gate_ref[1:2, lanes[head]])


def mix_kernel(self_ref, cross_ref, gate_ref, out_ref):
    for head in range(HEADS):
        z, yl = divmod(head, 2)
        lanes = slice(head * 128, (head + 1) * 128)
        out_ref[0, :, lanes] = (
            self_ref[seat(z, yl)].astype(jnp.float32) * gate_ref[0:1, lanes] + cross_ref[:, lanes]
        ).astype(jnp.bfloat16)


def shift(value, steps):
    pairs = [(source, (source + steps) % 8) for source in range(8)]
    return lax.ppermute(value, "cam", pairs)


def local(q_self, keys, values, q_cross, timestep, mod_table):
    rows, width = q_self.shape[1:]
    dim = width // HEADS
    scale = LOG2E / math.sqrt(dim)
    pieces, near = pl.pallas_call(
        pack_kernel,
        out_shape=(
            jax.ShapeDtypeStruct((2 * HEADS, 3 * rows, dim), jnp.bfloat16),
            jax.ShapeDtypeStruct((HEADS, 2 * rows, dim), jnp.bfloat16),
        ),
        in_specs=[pl.BlockSpec(memory_space=pltpu.HBM)] * 3,
        out_specs=(VMEM, VMEM),
        scratch_shapes=[pltpu.VMEM((rows, width), jnp.bfloat16)] * 3
        + [pltpu.SemaphoreType.DMA((3,))],
        compiler_params=grant(8),
        name="pack",
    )(*(pltpu.with_memory_space_constraint(x[0], pltpu.HBM) for x in (q_self, keys, values)))

    mine = lax.all_to_all(
        pieces, "sp", split_axis=0, concat_axis=0, axis_index_groups=owners(), tiled=True
    )
    left = shift(near, 1)
    right = shift(near, -1)
    gates = pl.pallas_call(
        pick_kernel,
        out_shape=jax.ShapeDtypeStruct((2, width), jnp.float32),
        in_specs=[pl.BlockSpec(memory_space=pltpu.SMEM), pl.BlockSpec(memory_space=pltpu.HBM)],
        out_specs=VMEM,
        scratch_shapes=[pltpu.SemaphoreType.DMA],
        compiler_params=grant(1),
        name="pick",
    )(timestep, pltpu.with_memory_space_constraint(mod_table, pltpu.HBM))
    cross = pl.pallas_call(
        functools.partial(cross_kernel, scale),
        out_shape=jax.ShapeDtypeStruct((rows, width), jnp.float32),
        in_specs=[VMEM] * 4,
        out_specs=VMEM,
        compiler_params=grant(8),
        name="cross",
    )(q_cross[0], left, right, gates)
    other = lax.ppermute(mine[:, : 2 * rows], "sp", [(i, i ^ 1) for i in range(64)])
    whole = lambda *shape: pl.BlockSpec(shape, lambda i, yh: (0,) * len(shape))
    part = pl.pallas_call(
        functools.partial(self_kernel, scale),
        out_shape=jax.ShapeDtypeStruct((HEADS, rows, dim), jnp.bfloat16),
        grid_spec=pltpu.PrefetchScalarGridSpec(
            num_scalar_prefetch=1,
            grid=(1,),
            in_specs=[whole(8, 2, 2, 3 * rows, dim), whole(8, 2, 2, 2 * rows, dim)],
            out_specs=whole(HEADS, rows, dim),
        ),
        compiler_params=grant(24),
        name="self",
    )(
        ((lax.axis_index("sp") // 4) % 2 ^ IN_YH)[None],
        mine.reshape(8, 2, 2, 3 * rows, dim),
        other.reshape(8, 2, 2, 2 * rows, dim),
    )
    own = lax.all_to_all(
        part, "sp", split_axis=0, concat_axis=0, axis_index_groups=half_owners(), tiled=True
    )
    return pl.pallas_call(
        mix_kernel,
        out_shape=jax.ShapeDtypeStruct((1, rows, width), jnp.bfloat16),
        in_specs=[VMEM] * 3,
        out_specs=VMEM,
        compiler_params=grant(8),
        name="mix",
    )(own, cross, gates)


def solution(mesh):
    block = P("cam", "sp", None)
    return jax.shard_map(
        local,
        mesh=mesh,
        in_specs=(block, block, block, block, P(), P()),
        out_specs=block,
        check_vma=False,
    )
```

```python
import functools
import math

import jax
import jax.numpy as jnp
from jax import lax
from jax.experimental import pallas as pl
from jax.experimental.pallas import tpu as pltpu
from jax.sharding import PartitionSpec as P

HEADS = 16
LOG2E = 1.4426950408889634

IN_Z, IN_YH, IN_YL = (5, 0, 1, 2, 3, 4, 6, 7), 1, 0
OUT_Z, OUT_YL = (4, 0, 1, 2, 3, 5, 6, 7), 1


def place(z, yh, yl, core):
    return ((z * 2 + yh) * 2 + yl) * 2 + core


def owners():
    return [
        [
            place(z, yh ^ IN_YH, yl ^ IN_YL, core)
            for z in IN_Z
            for yh in range(2)
            for yl in range(2)
        ]
        for core in range(2)
    ]


def half_owners():
    return [
        [place(z, yh, yl ^ OUT_YL, core) for z in OUT_Z for yl in range(2)]
        for yh in range(2)
        for core in range(2)
    ]


def seat(z, yl):
    return OUT_Z.index(z) * 2 + (yl ^ OUT_YL)


VMEM = pl.BlockSpec(memory_space=pltpu.VMEM)


def grant(mebibytes):
    return pltpu.CompilerParams(vmem_limit_bytes=mebibytes << 20)


def pack_kernel(
    q_hbm, k_hbm, v_hbm, piece_hbm, near_ref, piece_ref, q_ref, k_ref, v_ref, sems, out_sems
):
    rows = q_ref.shape[0]
    parts = (k_ref, v_ref, q_ref)
    copies = [
        pltpu.make_async_copy(source, target, sems.at[i])
        for i, (source, target) in enumerate(zip((k_hbm, v_hbm, q_hbm), parts))
    ]
    for copy in copies:
        copy.start()
    sent = []
    for i, (copy, part) in enumerate(zip(copies, parts)):
        copy.wait()
        to = slice(i * rows, (i + 1) * rows)
        for head in range(HEADS):
            z, yl = divmod(head, 2)
            line, side = IN_Z.index(z), yl ^ IN_YL
            block = part[:, head * 128 : (head + 1) * 128]
            piece_ref[i, line * 4 + side] = block
            piece_ref[i, line * 4 + 2 + side] = block
        sent.append(
            pltpu.make_async_copy(piece_ref.at[i], piece_hbm.at[:, to, :], out_sems.at[i])
        )
        sent[-1].start()
    for i, part in enumerate(parts[:2]):
        for head in range(HEADS):
            near_ref[head, i * rows : (i + 1) * rows, :] = part[:, head * 128 : (head + 1) * 128]
    for copy in sent:
        copy.wait()


def pick_kernel(step_ref, table_ref, out_ref, sem):
    copy = pltpu.make_async_copy(table_ref.at[step_ref[0]], out_ref, sem)
    copy.start()
    copy.wait()


def scores_of(query, key):
    return lax.dot_general(query, key, (((1,), (1,)), ((), ())), preferred_element_type=jnp.float32)


def self_kernel(scale, yh_ref, mine_ref, other_ref, out_ref):
    depths, _, across, depth, dim = mine_ref.shape
    part = depth // 3
    block = 4
    keys = [r[..., :part, :].reshape(-1, dim) for r in (mine_ref, other_ref)]
    values = [r[..., part : 2 * part, :].reshape(-1, dim) for r in (mine_ref, other_ref)]
    values = [jnp.concatenate([value, jnp.ones_like(value)], axis=1) for value in values]

    def scored(start):
        query = mine_ref[start : start + block, yh_ref[0], :, 2 * part :, :]
        query = query.reshape(block * across * part, dim)
        return [scores_of(query, key) for key in keys]

    ahead = scored(0)
    for start in range(0, depths, block):
        scores = ahead
        if start + block < depths:
            ahead = scored(start + block)
        peak = functools.reduce(
            jnp.maximum, [jnp.max(s, axis=1, keepdims=True) for s in scores]
        )
        weights = [jnp.exp2((s - peak) * scale).astype(jnp.bfloat16) for s in scores]
        summed = sum(
            jnp.dot(weight, value, preferred_element_type=jnp.float32)
            for weight, value in zip(weights, values)
        )
        mixed = (summed[:, :dim] / summed[:, dim:]).astype(jnp.bfloat16)
        for i in range(block * across):
            line, side = divmod(start * across + i, across)
            out_ref[seat(IN_Z[line], side ^ IN_YL)] = mixed[i * part : (i + 1) * part]


def mix_kernel(scale, self_ref, q_ref, left_ref, right_ref, gate_ref, out_ref):
    rows = q_ref.shape[0]
    both = lambda head, part: jnp.concatenate([left_ref[head, part], right_ref[head, part]], axis=0)
    lanes = [slice(head * 128, (head + 1) * 128) for head in range(HEADS)]
    scores = jnp.concatenate(
        [scores_of(q_ref[:, lanes[head]], both(head, slice(rows))) for head in range(HEADS)],
        axis=0,
    )
    weights = jnp.exp2((scores - jnp.max(scores, axis=1, keepdims=True)) * scale)
    inverse = 1.0 / jnp.sum(weights, axis=1, keepdims=True)
    weights = weights.astype(jnp.bfloat16)
    for head in range(HEADS):
        z, yl = divmod(head, 2)
        at = slice(head * rows, (head + 1) * rows)
        numerator = jnp.dot(
            weights[at], both(head, slice(rows, None)), preferred_element_type=jnp.float32
        )
        cross = numerator * (inverse[at] * gate_ref[1:2, lanes[head]])
        out_ref[0, :, lanes[head]] = (
            self_ref[seat(z, yl)].astype(jnp.float32) * gate_ref[0:1, lanes[head]] + cross
        ).astype(jnp.bfloat16)


def shift(value, steps):
    pairs = [(source, (source + steps) % 8) for source in range(8)]
    return lax.ppermute(value, "cam", pairs)


def local(q_self, keys, values, q_cross, timestep, mod_table):
    rows, width = q_self.shape[1:]
    dim = width // HEADS
    scale = LOG2E / math.sqrt(dim)
    pieces, near = pl.pallas_call(
        pack_kernel,
        out_shape=(
            jax.ShapeDtypeStruct((2 * HEADS, 3 * rows, dim), jnp.bfloat16),
            jax.ShapeDtypeStruct((HEADS, 2 * rows, dim), jnp.bfloat16),
        ),
        in_specs=[pl.BlockSpec(memory_space=pltpu.HBM)] * 3,
        out_specs=(pl.BlockSpec(memory_space=pltpu.HBM), VMEM),
        scratch_shapes=[pltpu.VMEM((3, 2 * HEADS, rows, dim), jnp.bfloat16)]
        + [pltpu.VMEM((rows, width), jnp.bfloat16)] * 3
        + [pltpu.SemaphoreType.DMA((3,)), pltpu.SemaphoreType.DMA((3,))],
        compiler_params=grant(8),
        name="pack",
    )(*(pltpu.with_memory_space_constraint(x[0], pltpu.HBM) for x in (q_self, keys, values)))

    mine = lax.all_to_all(
        pieces, "sp", split_axis=0, concat_axis=0, axis_index_groups=owners(), tiled=True
    )
    left = shift(near, 1)
    right = shift(near, -1)
    gates = pl.pallas_call(
        pick_kernel,
        out_shape=jax.ShapeDtypeStruct((2, width), jnp.float32),
        in_specs=[pl.BlockSpec(memory_space=pltpu.SMEM), pl.BlockSpec(memory_space=pltpu.HBM)],
        out_specs=VMEM,
        scratch_shapes=[pltpu.SemaphoreType.DMA],
        compiler_params=grant(1),
        name="pick",
    )(timestep, pltpu.with_memory_space_constraint(mod_table, pltpu.HBM))
    other = lax.ppermute(mine[:, : 2 * rows], "sp", [(i, i ^ 1) for i in range(64)])
    whole = lambda *shape: pl.BlockSpec(shape, lambda i, yh: (0,) * len(shape))
    part = pl.pallas_call(
        functools.partial(self_kernel, scale),
        out_shape=jax.ShapeDtypeStruct((HEADS, rows, dim), jnp.bfloat16),
        grid_spec=pltpu.PrefetchScalarGridSpec(
            num_scalar_prefetch=1,
            grid=(1,),
            in_specs=[whole(8, 2, 2, 3 * rows, dim), whole(8, 2, 2, 2 * rows, dim)],
            out_specs=whole(HEADS, rows, dim),
        ),
        compiler_params=grant(24),
        name="self",
    )(
        ((lax.axis_index("sp") // 4) % 2 ^ IN_YH)[None],
        mine.reshape(8, 2, 2, 3 * rows, dim),
        other.reshape(8, 2, 2, 2 * rows, dim),
    )
    own = lax.all_to_all(
        part, "sp", split_axis=0, concat_axis=0, axis_index_groups=half_owners(), tiled=True
    )
    return pl.pallas_call(
        functools.partial(mix_kernel, scale),
        out_shape=jax.ShapeDtypeStruct((1, rows, width), jnp.bfloat16),
        in_specs=[VMEM] * 5,
        out_specs=VMEM,
        compiler_params=grant(8),
        name="mix",
    )(own, q_cross[0], left, right, gates)


def solution(mesh):
    block = P("cam", "sp", None)
    return jax.shard_map(
        local,
        mesh=mesh,
        in_specs=(block, block, block, block, P(), P()),
        out_specs=block,
        check_vma=False,
    )
```

```python
import functools
import math

import jax
import jax.numpy as jnp
from jax import lax
from jax.experimental import pallas as pl
from jax.experimental.pallas import tpu as pltpu
from jax.sharding import PartitionSpec as P

HEADS = 16
LOG2E = 1.4426950408889634

IN_Z, IN_YH, IN_YL = (5, 0, 1, 2, 3, 4, 6, 7), 1, 0
OUT_Z, OUT_YL = (4, 0, 1, 2, 3, 5, 6, 7), 1


def place(z, yh, yl, core):
    return ((z * 2 + yh) * 2 + yl) * 2 + core


def owners():
    return [
        [
            place(z, yh ^ IN_YH, yl ^ IN_YL, core)
            for z in IN_Z
            for yh in range(2)
            for yl in range(2)
        ]
        for core in range(2)
    ]


def half_owners():
    return [
        [place(z, yh, yl ^ OUT_YL ^ yh, core) for z in OUT_Z for yl in range(2)]
        for yh in range(2)
        for core in range(2)
    ]


def seat(z, yl, flip):
    return OUT_Z.index(z) * 2 + (1 - flip if yl else flip)


VMEM = pl.BlockSpec(memory_space=pltpu.VMEM)


def grant(mebibytes):
    return pltpu.CompilerParams(vmem_limit_bytes=mebibytes << 20)


def pack_kernel(
    q_hbm, k_hbm, v_hbm, piece_hbm, near_ref, piece_ref, q_ref, k_ref, v_ref, sems, out_sems
):
    rows = q_ref.shape[0]
    parts = (k_ref, v_ref, q_ref)
    copies = [
        pltpu.make_async_copy(source, target, sems.at[i])
        for i, (source, target) in enumerate(zip((k_hbm, v_hbm, q_hbm), parts))
    ]
    for copy in copies:
        copy.start()
    sent = []
    for i, (copy, part) in enumerate(zip(copies, parts)):
        copy.wait()
        to = slice(i * rows, (i + 1) * rows)
        for head in range(HEADS):
            z, yl = divmod(head, 2)
            line, side = IN_Z.index(z), yl ^ IN_YL
            block = part[:, head * 128 : (head + 1) * 128]
            piece_ref[i, line * 4 + side] = block
            piece_ref[i, line * 4 + 2 + side] = block
        sent.append(
            pltpu.make_async_copy(piece_ref.at[i], piece_hbm.at[:, to, :], out_sems.at[i])
        )
        sent[-1].start()
    for i, part in enumerate(parts[:2]):
        for head in range(HEADS):
            near_ref[head, i * rows : (i + 1) * rows, :] = part[:, head * 128 : (head + 1) * 128]
    for copy in sent:
        copy.wait()


def pick_kernel(step_ref, table_ref, out_ref, sem):
    copy = pltpu.make_async_copy(table_ref.at[step_ref[0]], out_ref, sem)
    copy.start()
    copy.wait()


def scores_of(query, key):
    return lax.dot_general(query, key, (((1,), (1,)), ((), ())), preferred_element_type=jnp.float32)


def self_kernel(scale, yh_ref, mine_ref, other_ref, out_ref):
    depths, _, across, depth, dim = mine_ref.shape
    part = depth // 3
    block = 4
    keys = [r[..., :part, :].reshape(-1, dim) for r in (mine_ref, other_ref)]
    values = [r[..., part : 2 * part, :].reshape(-1, dim) for r in (mine_ref, other_ref)]
    values = [jnp.concatenate([value, jnp.ones_like(value)], axis=1) for value in values]

    def scored(start):
        query = mine_ref[start : start + block, yh_ref[0], :, 2 * part :, :]
        query = query.reshape(block * across * part, dim)
        return [scores_of(query, key) for key in keys]

    ahead = scored(0)
    for start in range(0, depths, block):
        scores = ahead
        if start + block < depths:
            ahead = scored(start + block)
        peak = functools.reduce(
            jnp.maximum, [jnp.max(s, axis=1, keepdims=True) for s in scores]
        )
        weights = [jnp.exp2((s - peak) * scale).astype(jnp.bfloat16) for s in scores]
        summed = sum(
            jnp.dot(weight, value, preferred_element_type=jnp.float32)
            for weight, value in zip(weights, values)
        )
        mixed = (summed[:, :dim] / summed[:, dim:]).astype(jnp.bfloat16)
        for i in range(block * across):
            line, side = divmod(start * across + i, across)
            out_ref[seat(IN_Z[line], side ^ IN_YL, yh_ref[0])] = mixed[i * part : (i + 1) * part]


def mix_kernel(scale, flip_ref, self_ref, q_ref, left_ref, right_ref, gate_ref, out_ref):
    rows = q_ref.shape[0]
    both = lambda head, part: jnp.concatenate([left_ref[head, part], right_ref[head, part]], axis=0)
    lanes = [slice(head * 128, (head + 1) * 128) for head in range(HEADS)]
    scores = jnp.concatenate(
        [scores_of(q_ref[:, lanes[head]], both(head, slice(rows))) for head in range(HEADS)],
        axis=0,
    )
    weights = jnp.exp2((scores - jnp.max(scores, axis=1, keepdims=True)) * scale)
    inverse = 1.0 / jnp.sum(weights, axis=1, keepdims=True)
    weights = weights.astype(jnp.bfloat16)
    for head in range(HEADS):
        z, yl = divmod(head, 2)
        at = slice(head * rows, (head + 1) * rows)
        numerator = jnp.dot(
            weights[at], both(head, slice(rows, None)), preferred_element_type=jnp.float32
        )
        cross = numerator * (inverse[at] * gate_ref[1:2, lanes[head]])
        out_ref[0, :, lanes[head]] = (
            self_ref[seat(z, yl, flip_ref[0])].astype(jnp.float32) * gate_ref[0:1, lanes[head]] + cross
        ).astype(jnp.bfloat16)


def shift(value, steps):
    pairs = [(source, (source + steps) % 8) for source in range(8)]
    return lax.ppermute(value, "cam", pairs)


def local(q_self, keys, values, q_cross, timestep, mod_table):
    rows, width = q_self.shape[1:]
    dim = width // HEADS
    scale = LOG2E / math.sqrt(dim)
    lower = (1 - (lax.axis_index("sp") // 4) % 2)[None]
    pieces, near = pl.pallas_call(
        pack_kernel,
        out_shape=(
            jax.ShapeDtypeStruct((2 * HEADS, 3 * rows, dim), jnp.bfloat16),
            jax.ShapeDtypeStruct((HEADS, 2 * rows, dim), jnp.bfloat16),
        ),
        in_specs=[pl.BlockSpec(memory_space=pltpu.HBM)] * 3,
        out_specs=(pl.BlockSpec(memory_space=pltpu.HBM), VMEM),
        scratch_shapes=[pltpu.VMEM((3, 2 * HEADS, rows, dim), jnp.bfloat16)]
        + [pltpu.VMEM((rows, width), jnp.bfloat16)] * 3
        + [pltpu.SemaphoreType.DMA((3,)), pltpu.SemaphoreType.DMA((3,))],
        compiler_params=grant(8),
        name="pack",
    )(*(pltpu.with_memory_space_constraint(x[0], pltpu.HBM) for x in (q_self, keys, values)))

    mine = lax.all_to_all(
        pieces, "sp", split_axis=0, concat_axis=0, axis_index_groups=owners(), tiled=True
    )
    left = shift(near, 1)
    right = shift(near, -1)
    gates = pl.pallas_call(
        pick_kernel,
        out_shape=jax.ShapeDtypeStruct((2, width), jnp.float32),
        in_specs=[pl.BlockSpec(memory_space=pltpu.SMEM), pl.BlockSpec(memory_space=pltpu.HBM)],
        out_specs=VMEM,
        scratch_shapes=[pltpu.SemaphoreType.DMA],
        compiler_params=grant(1),
        name="pick",
    )(timestep, pltpu.with_memory_space_constraint(mod_table, pltpu.HBM))
    other = lax.ppermute(mine[:, : 2 * rows], "sp", [(i, i ^ 1) for i in range(64)])
    whole = lambda *shape: pl.BlockSpec(shape, lambda i, yh: (0,) * len(shape))
    part = pl.pallas_call(
        functools.partial(self_kernel, scale),
        out_shape=jax.ShapeDtypeStruct((HEADS, rows, dim), jnp.bfloat16),
        grid_spec=pltpu.PrefetchScalarGridSpec(
            num_scalar_prefetch=1,
            grid=(1,),
            in_specs=[whole(8, 2, 2, 3 * rows, dim), whole(8, 2, 2, 2 * rows, dim)],
            out_specs=whole(HEADS, rows, dim),
        ),
        compiler_params=grant(24),
        name="self",
    )(
        lower,
        mine.reshape(8, 2, 2, 3 * rows, dim),
        other.reshape(8, 2, 2, 2 * rows, dim),
    )
    own = lax.all_to_all(
        part, "sp", split_axis=0, concat_axis=0, axis_index_groups=half_owners(), tiled=True
    )
    return pl.pallas_call(
        functools.partial(mix_kernel, scale),
        out_shape=jax.ShapeDtypeStruct((1, rows, width), jnp.bfloat16),
        in_specs=[pl.BlockSpec(memory_space=pltpu.SMEM)] + [VMEM] * 5,
        out_specs=VMEM,
        compiler_params=grant(8),
        name="mix",
    )(lower, own, q_cross[0], left, right, gates)


def solution(mesh):
    block = P("cam", "sp", None)
    return jax.shard_map(
        local,
        mesh=mesh,
        in_specs=(block, block, block, block, P(), P()),
        out_specs=block,
        check_vma=False,
    )
```

```python
import functools
import math

import jax
import jax.numpy as jnp
from jax import lax
from jax.experimental import pallas as pl
from jax.experimental.pallas import tpu as pltpu
from jax.sharding import PartitionSpec as P

HEADS = 16
LOG2E = 1.4426950408889634

IN_Z, IN_YH, IN_YL = (5, 0, 1, 2, 3, 4, 6, 7), 1, 0
OUT_Z, OUT_YL = ((4, 0, 1, 2, 3, 5, 6, 7), (5, 0, 1, 2, 3, 4, 6, 7)), 1


def place(z, yh, yl, core):
    return ((z * 2 + yh) * 2 + yl) * 2 + core


def owners():
    return [
        [
            place(z, yh ^ IN_YH, yl ^ IN_YL, core)
            for z in IN_Z
            for yh in range(2)
            for yl in range(2)
        ]
        for core in range(2)
    ]


def half_owners():
    return [
        [place(z, yh, yl ^ OUT_YL ^ yh, core) for z in OUT_Z[yh] for yl in range(2)]
        for yh in range(2)
        for core in range(2)
    ]


def seat(z, yl, flip):
    below, above = (order.index(z) for order in OUT_Z)
    return (above + (below - above) * flip) * 2 + (1 - flip if yl else flip)


VMEM = pl.BlockSpec(memory_space=pltpu.VMEM)


def grant(mebibytes):
    return pltpu.CompilerParams(vmem_limit_bytes=mebibytes << 20)


def pack_kernel(
    q_hbm, k_hbm, v_hbm, piece_hbm, near_ref, piece_ref, q_ref, k_ref, v_ref, sems, out_sems
):
    rows = q_ref.shape[0]
    parts = (k_ref, v_ref, q_ref)
    copies = [
        pltpu.make_async_copy(source, target, sems.at[i])
        for i, (source, target) in enumerate(zip((k_hbm, v_hbm, q_hbm), parts))
    ]
    for copy in copies:
        copy.start()
    sent = []
    for i, (copy, part) in enumerate(zip(copies, parts)):
        copy.wait()
        to = slice(i * rows, (i + 1) * rows)
        for head in range(HEADS):
            z, yl = divmod(head, 2)
            line, side = IN_Z.index(z), yl ^ IN_YL
            block = part[:, head * 128 : (head + 1) * 128]
            piece_ref[i, line * 4 + side] = block
            piece_ref[i, line * 4 + 2 + side] = block
        sent.append(
            pltpu.make_async_copy(piece_ref.at[i], piece_hbm.at[:, to, :], out_sems.at[i])
        )
        sent[-1].start()
    for i, part in enumerate(parts[:2]):
        for head in range(HEADS):
            near_ref[head, i * rows : (i + 1) * rows, :] = part[:, head * 128 : (head + 1) * 128]
    for copy in sent:
        copy.wait()


def pick_kernel(step_ref, table_ref, out_ref, sem):
    copy = pltpu.make_async_copy(table_ref.at[step_ref[0]], out_ref, sem)
    copy.start()
    copy.wait()


def scores_of(query, key):
    return lax.dot_general(query, key, (((1,), (1,)), ((), ())), preferred_element_type=jnp.float32)


def self_kernel(scale, yh_ref, mine_ref, other_ref, out_ref):
    depths, _, across, depth, dim = mine_ref.shape
    part = depth // 3
    block = 4
    keys = [r[..., :part, :].reshape(-1, dim) for r in (mine_ref, other_ref)]
    values = [r[..., part : 2 * part, :].reshape(-1, dim) for r in (mine_ref, other_ref)]
    values = [jnp.concatenate([value, jnp.ones_like(value)], axis=1) for value in values]

    def scored(start):
        query = mine_ref[start : start + block, yh_ref[0], :, 2 * part :, :]
        query = query.reshape(block * across * part, dim)
        return [scores_of(query, key) for key in keys]

    ahead = scored(0)
    for start in range(0, depths, block):
        scores = ahead
        if start + block < depths:
            ahead = scored(start + block)
        peak = functools.reduce(
            jnp.maximum, [jnp.max(s, axis=1, keepdims=True) for s in scores]
        )
        weights = [jnp.exp2((s - peak) * scale).astype(jnp.bfloat16) for s in scores]
        summed = sum(
            jnp.dot(weight, value, preferred_element_type=jnp.float32)
            for weight, value in zip(weights, values)
        )
        mixed = (summed[:, :dim] / summed[:, dim:]).astype(jnp.bfloat16)
        for i in range(block * across):
            line, side = divmod(start * across + i, across)
            out_ref[seat(IN_Z[line], side ^ IN_YL, yh_ref[0])] = mixed[i * part : (i + 1) * part]


def mix_kernel(scale, flip_ref, self_ref, q_ref, left_ref, right_ref, gate_ref, out_ref):
    rows = q_ref.shape[0]
    both = lambda head, part: jnp.concatenate([left_ref[head, part], right_ref[head, part]], axis=0)
    lanes = [slice(head * 128, (head + 1) * 128) for head in range(HEADS)]
    scores = jnp.concatenate(
        [scores_of(q_ref[:, lanes[head]], both(head, slice(rows))) for head in range(HEADS)],
        axis=0,
    )
    weights = jnp.exp2((scores - jnp.max(scores, axis=1, keepdims=True)) * scale)
    inverse = 1.0 / jnp.sum(weights, axis=1, keepdims=True)
    weights = weights.astype(jnp.bfloat16)
    for head in range(HEADS):
        z, yl = divmod(head, 2)
        at = slice(head * rows, (head + 1) * rows)
        numerator = jnp.dot(
            weights[at], both(head, slice(rows, None)), preferred_element_type=jnp.float32
        )
        cross = numerator * (inverse[at] * gate_ref[1:2, lanes[head]])
        out_ref[0, :, lanes[head]] = (
            self_ref[seat(z, yl, flip_ref[0])].astype(jnp.float32) * gate_ref[0:1, lanes[head]] + cross
        ).astype(jnp.bfloat16)


def shift(value, steps):
    pairs = [(source, (source + steps) % 8) for source in range(8)]
    return lax.ppermute(value, "cam", pairs)


def local(q_self, keys, values, q_cross, timestep, mod_table):
    rows, width = q_self.shape[1:]
    dim = width // HEADS
    scale = LOG2E / math.sqrt(dim)
    lower = (1 - (lax.axis_index("sp") // 4) % 2)[None]
    pieces, near = pl.pallas_call(
        pack_kernel,
        out_shape=(
            jax.ShapeDtypeStruct((2 * HEADS, 3 * rows, dim), jnp.bfloat16),
            jax.ShapeDtypeStruct((HEADS, 2 * rows, dim), jnp.bfloat16),
        ),
        in_specs=[pl.BlockSpec(memory_space=pltpu.HBM)] * 3,
        out_specs=(pl.BlockSpec(memory_space=pltpu.HBM), VMEM),
        scratch_shapes=[pltpu.VMEM((3, 2 * HEADS, rows, dim), jnp.bfloat16)]
        + [pltpu.VMEM((rows, width), jnp.bfloat16)] * 3
        + [pltpu.SemaphoreType.DMA((3,)), pltpu.SemaphoreType.DMA((3,))],
        compiler_params=grant(8),
        name="pack",
    )(*(pltpu.with_memory_space_constraint(x[0], pltpu.HBM) for x in (q_self, keys, values)))

    mine = lax.all_to_all(
        pieces, "sp", split_axis=0, concat_axis=0, axis_index_groups=owners(), tiled=True
    )
    left = shift(near, 1)
    right = shift(near, -1)
    gates = pl.pallas_call(
        pick_kernel,
        out_shape=jax.ShapeDtypeStruct((2, width), jnp.float32),
        in_specs=[pl.BlockSpec(memory_space=pltpu.SMEM), pl.BlockSpec(memory_space=pltpu.HBM)],
        out_specs=VMEM,
        scratch_shapes=[pltpu.SemaphoreType.DMA],
        compiler_params=grant(1),
        name="pick",
    )(timestep, pltpu.with_memory_space_constraint(mod_table, pltpu.HBM))
    other = lax.ppermute(mine[:, : 2 * rows], "sp", [(i, i ^ 1) for i in range(64)])
    whole = lambda *shape: pl.BlockSpec(shape, lambda i, yh: (0,) * len(shape))
    part = pl.pallas_call(
        functools.partial(self_kernel, scale),
        out_shape=jax.ShapeDtypeStruct((HEADS, rows, dim), jnp.bfloat16),
        grid_spec=pltpu.PrefetchScalarGridSpec(
            num_scalar_prefetch=1,
            grid=(1,),
            in_specs=[whole(8, 2, 2, 3 * rows, dim), whole(8, 2, 2, 2 * rows, dim)],
            out_specs=whole(HEADS, rows, dim),
        ),
        compiler_params=grant(24),
        name="self",
    )(
        lower,
        mine.reshape(8, 2, 2, 3 * rows, dim),
        other.reshape(8, 2, 2, 2 * rows, dim),
    )
    own = lax.all_to_all(
        part, "sp", split_axis=0, concat_axis=0, axis_index_groups=half_owners(), tiled=True
    )
    return pl.pallas_call(
        functools.partial(mix_kernel, scale),
        out_shape=jax.ShapeDtypeStruct((1, rows, width), jnp.bfloat16),
        in_specs=[pl.BlockSpec(memory_space=pltpu.SMEM)] + [VMEM] * 5,
        out_specs=VMEM,
        compiler_params=grant(8),
        name="mix",
    )(lower, own, q_cross[0], left, right, gates)


def solution(mesh):
    block = P("cam", "sp", None)
    return jax.shard_map(
        local,
        mesh=mesh,
        in_specs=(block, block, block, block, P(), P()),
        out_specs=block,
        check_vma=False,
    )
```

```python
import functools
import math

import jax
import jax.numpy as jnp
from jax import lax
from jax.experimental import pallas as pl
from jax.experimental.pallas import tpu as pltpu
from jax.sharding import PartitionSpec as P

HEADS = 16
LOG2E = 1.4426950408889634

IN_Z, IN_YH, IN_YL = (5, 0, 1, 2, 3, 4, 6, 7), 1, 0
OUT_Z, OUT_YL = ((4, 0, 1, 2, 3, 5, 6, 7), (5, 0, 1, 2, 3, 4, 6, 7)), 1


def place(z, yh, yl, core):
    return ((z * 2 + yh) * 2 + yl) * 2 + core


def owners():
    return [
        [
            place(z, yh ^ IN_YH, yl ^ IN_YL, core)
            for z in IN_Z
            for yh in range(2)
            for yl in range(2)
        ]
        for core in range(2)
    ]


def half_owners():
    return [
        [place(z, yh, yl ^ OUT_YL ^ yh, core) for z in OUT_Z[yh] for yl in range(2)]
        for yh in range(2)
        for core in range(2)
    ]


def seat(z, yl, flip):
    below, above = (order.index(z) for order in OUT_Z)
    return (above + (below - above) * flip) * 2 + (1 - flip if yl else flip)


VMEM = pl.BlockSpec(memory_space=pltpu.VMEM)


def grant(mebibytes):
    return pltpu.CompilerParams(vmem_limit_bytes=mebibytes << 20)


def pack_kernel(
    q_hbm, k_hbm, v_hbm, piece_hbm, near_ref, piece_ref, q_ref, k_ref, v_ref, sems, out_sems
):
    rows = q_ref.shape[0]
    parts = (k_ref, v_ref, q_ref)
    copies = [
        pltpu.make_async_copy(source, target, sems.at[i])
        for i, (source, target) in enumerate(zip((k_hbm, v_hbm, q_hbm), parts))
    ]
    for copy in copies:
        copy.start()
    sent = []
    for i, (copy, part) in enumerate(zip(copies, parts)):
        copy.wait()
        to = slice(i * rows, (i + 1) * rows)
        for head in range(HEADS):
            z, yl = divmod(head, 2)
            line, side = IN_Z.index(z), yl ^ IN_YL
            block = part[:, head * 128 : (head + 1) * 128]
            piece_ref[i, line * 4 + side] = block
            piece_ref[i, line * 4 + 2 + side] = block
        sent.append(
            pltpu.make_async_copy(piece_ref.at[i], piece_hbm.at[:, to, :], out_sems.at[i])
        )
        sent[-1].start()
    for i, part in enumerate(parts[:2]):
        for head in range(HEADS):
            near_ref[head, i * rows : (i + 1) * rows, :] = part[:, head * 128 : (head + 1) * 128]
    for copy in sent:
        copy.wait()


def pick_kernel(step_ref, table_ref, out_ref, sem):
    copy = pltpu.make_async_copy(table_ref.at[step_ref[0]], out_ref, sem)
    copy.start()
    copy.wait()


def scores_of(query, key):
    return lax.dot_general(query, key, (((1,), (1,)), ((), ())), preferred_element_type=jnp.float32)


def self_kernel(scale, yh_ref, mine_ref, other_ref, out_ref):
    depths, _, across, depth, dim = mine_ref.shape
    part = depth // 3
    block = 4
    keys = [r[..., :part, :].reshape(-1, dim) for r in (mine_ref, other_ref)]
    values = [r[..., part : 2 * part, :].reshape(-1, dim) for r in (mine_ref, other_ref)]
    values = [jnp.concatenate([value, jnp.ones_like(value)], axis=1) for value in values]

    def scored(start):
        query = mine_ref[start : start + block, yh_ref[0], :, 2 * part :, :]
        query = query.reshape(block * across * part, dim)
        return [scores_of(query, key) for key in keys]

    ahead = scored(0)
    for start in range(0, depths, block):
        scores = ahead
        if start + block < depths:
            ahead = scored(start + block)
        peak = functools.reduce(
            jnp.maximum, [jnp.max(s, axis=1, keepdims=True) for s in scores]
        )
        weights = [jnp.exp2((s - peak) * scale).astype(jnp.bfloat16) for s in scores]
        summed = sum(
            jnp.dot(weight, value, preferred_element_type=jnp.float32)
            for weight, value in zip(weights, values)
        )
        mixed = (summed[:, :dim] / summed[:, dim:]).astype(jnp.bfloat16)
        for i in range(block * across):
            line, side = divmod(start * across + i, across)
            out_ref[seat(IN_Z[line], side ^ IN_YL, yh_ref[0])] = mixed[i * part : (i + 1) * part]


def cross_kernel(scale, q_ref, left_ref, right_ref, gate_ref, out_ref):
    rows = q_ref.shape[0]
    both = lambda head, part: jnp.concatenate([left_ref[head, part], right_ref[head, part]], axis=0)
    lanes = [slice(head * 128, (head + 1) * 128) for head in range(HEADS)]
    scores = jnp.concatenate(
        [scores_of(q_ref[:, lanes[head]], both(head, slice(rows))) for head in range(HEADS)],
        axis=0,
    )
    weights = jnp.exp2((scores - jnp.max(scores, axis=1, keepdims=True)) * scale)
    inverse = 1.0 / jnp.sum(weights, axis=1, keepdims=True)
    weights = weights.astype(jnp.bfloat16)
    for head in range(HEADS):
        at = slice(head * rows, (head + 1) * rows)
        numerator = jnp.dot(
            weights[at], both(head, slice(rows, None)), preferred_element_type=jnp.float32
        )
        out_ref[:, lanes[head]] = numerator * (inverse[at] * gate_ref[1:2, lanes[head]])


def mix_kernel(flip_ref, self_ref, cross_ref, gate_ref, out_ref):
    for head in range(HEADS):
        z, yl = divmod(head, 2)
        lanes = slice(head * 128, (head + 1) * 128)
        out_ref[0, :, lanes] = (
            self_ref[seat(z, yl, flip_ref[0])].astype(jnp.float32) * gate_ref[0:1, lanes]
            + cross_ref[:, lanes]
        ).astype(jnp.bfloat16)


def shift(value, steps):
    pairs = [(source, (source + steps) % 8) for source in range(8)]
    return lax.ppermute(value, "cam", pairs)


def local(q_self, keys, values, q_cross, timestep, mod_table):
    rows, width = q_self.shape[1:]
    dim = width // HEADS
    scale = LOG2E / math.sqrt(dim)
    lower = (1 - (lax.axis_index("sp") // 4) % 2)[None]
    pieces, near = pl.pallas_call(
        pack_kernel,
        out_shape=(
            jax.ShapeDtypeStruct((2 * HEADS, 3 * rows, dim), jnp.bfloat16),
            jax.ShapeDtypeStruct((HEADS, 2 * rows, dim), jnp.bfloat16),
        ),
        in_specs=[pl.BlockSpec(memory_space=pltpu.HBM)] * 3,
        out_specs=(pl.BlockSpec(memory_space=pltpu.HBM), VMEM),
        scratch_shapes=[pltpu.VMEM((3, 2 * HEADS, rows, dim), jnp.bfloat16)]
        + [pltpu.VMEM((rows, width), jnp.bfloat16)] * 3
        + [pltpu.SemaphoreType.DMA((3,)), pltpu.SemaphoreType.DMA((3,))],
        compiler_params=grant(8),
        name="pack",
    )(*(pltpu.with_memory_space_constraint(x[0], pltpu.HBM) for x in (q_self, keys, values)))

    mine = lax.all_to_all(
        pieces, "sp", split_axis=0, concat_axis=0, axis_index_groups=owners(), tiled=True
    )
    left = shift(near, 1)
    right = shift(near, -1)
    gates = pl.pallas_call(
        pick_kernel,
        out_shape=jax.ShapeDtypeStruct((2, width), jnp.float32),
        in_specs=[pl.BlockSpec(memory_space=pltpu.SMEM), pl.BlockSpec(memory_space=pltpu.HBM)],
        out_specs=VMEM,
        scratch_shapes=[pltpu.SemaphoreType.DMA],
        compiler_params=grant(1),
        name="pick",
    )(timestep, pltpu.with_memory_space_constraint(mod_table, pltpu.HBM))
    cross = pl.pallas_call(
        functools.partial(cross_kernel, scale),
        out_shape=jax.ShapeDtypeStruct((rows, width), jnp.float32),
        in_specs=[VMEM] * 4,
        out_specs=VMEM,
        compiler_params=grant(8),
        name="cross",
    )(q_cross[0], left, right, gates)
    other = lax.ppermute(mine[:, : 2 * rows], "sp", [(i, i ^ 1) for i in range(64)])
    whole = lambda *shape: pl.BlockSpec(shape, lambda i, yh: (0,) * len(shape))
    part = pl.pallas_call(
        functools.partial(self_kernel, scale),
        out_shape=jax.ShapeDtypeStruct((HEADS, rows, dim), jnp.bfloat16),
        grid_spec=pltpu.PrefetchScalarGridSpec(
            num_scalar_prefetch=1,
            grid=(1,),
            in_specs=[whole(8, 2, 2, 3 * rows, dim), whole(8, 2, 2, 2 * rows, dim)],
            out_specs=whole(HEADS, rows, dim),
        ),
        compiler_params=grant(24),
        name="self",
    )(
        lower,
        mine.reshape(8, 2, 2, 3 * rows, dim),
        other.reshape(8, 2, 2, 2 * rows, dim),
    )
    own = lax.all_to_all(
        part, "sp", split_axis=0, concat_axis=0, axis_index_groups=half_owners(), tiled=True
    )
    return pl.pallas_call(
        mix_kernel,
        out_shape=jax.ShapeDtypeStruct((1, rows, width), jnp.bfloat16),
        in_specs=[pl.BlockSpec(memory_space=pltpu.SMEM)] + [VMEM] * 3,
        out_specs=VMEM,
        compiler_params=grant(8),
        name="mix",
    )(lower, own, cross, gates)


def solution(mesh):
    block = P("cam", "sp", None)
    return jax.shard_map(
        local,
        mesh=mesh,
        in_specs=(block, block, block, block, P(), P()),
        out_specs=block,
        check_vma=False,
    )
```
